32 devices in a mesh: section: 4 (over z), tp: 8 (over y, x, core).
Axes of the slice: x: 2, y: 2, z: 4, core: 2. Of those that a mesh axis runs over, the one named last changes fastest.
Arguments:
- hidden_entering: bfloat16 [4, 16, 8192], P('section', None, 'tp'), may hold values from -6 to 6
- layer_norm_gain: bfloat16 [4, 8192], P('section'), may hold values from 0.25 to 1.75
- query_matrix: bfloat16 [4, 8192, 4096], P('section', None, 'tp'), may hold values from -0.0625 to 0.0625
- output_matrix: bfloat16 [4, 4096, 8192], P('section', 'tp'), may hold values from -0.09375 to 0.09375
- adapter_down_weight: bfloat16 [4, 4, 64, 8192], P('section', None, 'tp'), may hold values from -0.0625 to 0.0625
- adapter_up_weight: bfloat16 [4, 4, 64, 4096], P('section', None, None, 'tp'), may hold values from -0.75 to 0.75
- key_value_cache: bfloat16 [4, 3, 16, 32, 1024], P('section', None, 'tp')
- adapter_index: int32 [4, 16], replicated, may hold values from 0 to 3
- cached_lengths: int32 [4, 16], replicated, may hold values from 1 to 32, as said below
Outputs:
- section_out: bfloat16 [4, 3, 16, 8192], P('section', None, None, 'tp')
The draws below stay inside these ranges and needn't reach their ends.
Inputs may be any that keep to these rules, and one draw needn't show every extreme that they name: `cached_lengths`: in every group some request uses all 32 cached positions.
All inputs are finite; a program needn't handle non-finite values.
Results may differ from the reference program's by a relative error of at most 0.03.
Values may be sent and summed in bfloat16 or wider, within the bound.
A program may use at most 64 MiB of HBM per device.

```python
import jax
import jax.numpy as jnp
from jax import lax

MODEL_WIDTH = 8192
HD = 128
HEADS = 32
KVH = 4
ADAPTER_RANK = 64
ADAPTER_COUNT = 4
CTX = 32
TICKS = 3
GROUP_REQUESTS = 16
QUERY_WIDTH = 4096
SECTION_COUNT = 4
N_TP = 8


def draw_cached_lengths(key, part):
    first, second = jax.random.split(jax.random.fold_in(key, 11))
    request_lengths = jax.random.randint(first, (SECTION_COUNT, GROUP_REQUESTS), 1, CTX + 1)
    spot = jax.random.randint(second, (SECTION_COUNT, 1), 0, GROUP_REQUESTS)
    return jnp.where(jnp.arange(GROUP_REQUESTS)[None, :] == spot, CTX, request_lengths).astype(jnp.int32)


def draw_key_value_cache(key, part):
    first = jax.random.fold_in(jax.random.fold_in(key, 23), 0)
    values = jax.random.normal(first, (SECTION_COUNT, TICKS, GROUP_REQUESTS, CTX, 2 * KVH * HD), jnp.float32)
    return values.astype(jnp.bfloat16)


def plant(entries, rng, least, largest):
    index_at = [jax.random.randint(jax.random.fold_in(rng, axis), (), 0, length) for axis, length in enumerate(entries.shape)]
    widest = entries.shape.index(max(entries.shape))
    beside = index_at[:widest] + [(index_at[widest] + 1) % entries.shape[widest]] + index_at[widest + 1:]
    return entries.at[tuple(index_at)].set(least).at[tuple(beside)].set(largest)


def level_of(stream_key, shape, pieces, least, largest):
    level, own = 1.0, jax.random.fold_in(stream_key, 6)
    for dim, shards_of in pieces:
        draws = jnp.exp(jax.random.uniform(jax.random.fold_in(own, dim), (shards_of,), jnp.float32, least / len(pieces), largest / len(pieces)))
        level = level * jnp.repeat(draws, shape[dim] // shards_of).reshape([-1 if axis == dim else 1 for axis in range(len(shape))])
    return level


def bell_draw(stream_key, dims, width, limit, pieces=(), kind=jnp.bfloat16):
    values = jax.random.normal(stream_key, dims, jnp.float32) * width
    if len(pieces) > 0:
        values = level_of(stream_key, dims, pieces, -0.22, 0.18) * values
    return jnp.clip(values, min=-limit, max=limit).astype(kind)


def setup_inputs(seed: int = 0) -> dict:
    streams_of = jax.random.split(jax.random.key(seed), 10)
    hidden_entering = bell_draw(streams_of[0], (SECTION_COUNT, GROUP_REQUESTS, MODEL_WIDTH), 1.0, 6.0, ((0, 4), (2, 8)))
    layer_norm_gain = jnp.clip(1.0 + 0.15 * jax.random.normal(streams_of[1], (SECTION_COUNT, MODEL_WIDTH), jnp.float32), 0.25, 1.75).astype(jnp.bfloat16)
    query_matrix = bell_draw(streams_of[2], (SECTION_COUNT, MODEL_WIDTH, QUERY_WIDTH), MODEL_WIDTH ** -0.5, 0.0625, ((0, 4), (2, 8)))
    output_matrix = bell_draw(streams_of[3], (SECTION_COUNT, QUERY_WIDTH, MODEL_WIDTH), QUERY_WIDTH ** -0.5, 0.09375, ((0, 4), (1, 8)))
    adapter_down_weight = bell_draw(streams_of[4], (SECTION_COUNT, ADAPTER_COUNT, ADAPTER_RANK, MODEL_WIDTH), MODEL_WIDTH ** -0.5, 0.0625, ((0, 4), (2, 8)))
    adapter_up_weight = bell_draw(streams_of[5], (SECTION_COUNT, ADAPTER_COUNT, ADAPTER_RANK, QUERY_WIDTH), ADAPTER_RANK ** -0.5, 0.75, ((0, 4), (3, 8)))
    key_value_cache = draw_key_value_cache(jax.random.fold_in(streams_of[9], 71), 0)
    adapter_index = plant(jax.random.randint(streams_of[7], (SECTION_COUNT, GROUP_REQUESTS), 0, ADAPTER_COUNT), jax.random.fold_in(streams_of[7], 1), 0, ADAPTER_COUNT - 1).astype(jnp.int32)
    cached_lengths = draw_cached_lengths(jax.random.fold_in(streams_of[9], 71), 0)
    return dict(hidden_entering=hidden_entering, layer_norm_gain=layer_norm_gain, query_matrix=query_matrix, output_matrix=output_matrix, adapter_down_weight=adapter_down_weight, adapter_up_weight=adapter_up_weight, key_value_cache=key_value_cache, adapter_index=adapter_index, cached_lengths=cached_lengths)


adapter_scale = 2.0

def layer_index(args):
    x, gain, wq, wo, down_matrix, up_matrix, cache, request_adapters, request_lengths = args
    xf = x.astype(jnp.float32)
    inv = lax.rsqrt(lax.optimization_barrier(jnp.mean(xf * xf, axis=-1, keepdims=True)) + 1e-05)
    xn = (xf * inv * gain.astype(jnp.float32)[None, :]).astype(jnp.bfloat16)
    base_query = jnp.dot(xn, wq, preferred_element_type=jnp.float32)
    onehot = (request_adapters[:, None] == jnp.arange(ADAPTER_COUNT, dtype=jnp.int32)[None, :]).astype(jnp.float32)
    u_all = jnp.dot(xn, down_matrix.reshape(ADAPTER_COUNT * ADAPTER_RANK, MODEL_WIDTH).T, preferred_element_type=jnp.float32)
    u_all = u_all.reshape(GROUP_REQUESTS, ADAPTER_COUNT, ADAPTER_RANK)
    u_sel = lax.optimization_barrier(jnp.sum(u_all * onehot[:, :, None], axis=1)).astype(jnp.bfloat16)
    spread_rows = (onehot.astype(jnp.bfloat16)[:, :, None] * u_sel[:, None, :]).reshape(GROUP_REQUESTS, ADAPTER_COUNT * ADAPTER_RANK)
    adapter_delta = jnp.dot(spread_rows, up_matrix.reshape(ADAPTER_COUNT * ADAPTER_RANK, QUERY_WIDTH), preferred_element_type=jnp.float32)
    query_rows = (base_query + adapter_scale * adapter_delta).astype(jnp.bfloat16)
    group = HEADS // KVH
    qh = query_rows.reshape(GROUP_REQUESTS, KVH, group, HD).astype(jnp.float32)
    keys = cache[:, :, :KVH * HD].reshape(GROUP_REQUESTS, CTX, KVH, HD).astype(jnp.float32)
    values = cache[:, :, KVH * HD:].reshape(GROUP_REQUESTS, CTX, KVH, HD).astype(jnp.float32)
    scores = jnp.einsum('rkgh,rckh->rkgc', qh, keys) * HD ** (-0.5)
    valid = (jnp.arange(CTX, dtype=jnp.int32)[None, :] < request_lengths[:, None])[:, None, None, :]
    scores = jnp.where(valid, scores, -1e+30)
    top = lax.optimization_barrier(jnp.max(scores, axis=-1, keepdims=True))
    expo = jnp.where(valid, jnp.exp(scores - top), 0.0)
    weights = (expo / lax.optimization_barrier(jnp.sum(expo, axis=-1, keepdims=True))).astype(jnp.bfloat16)
    attn = jnp.einsum('rkgc,rckh->rkgh', weights.astype(jnp.float32), values)
    attn = attn.reshape(GROUP_REQUESTS, QUERY_WIDTH).astype(jnp.bfloat16)
    block_list = attn.reshape(GROUP_REQUESTS, N_TP, QUERY_WIDTH // N_TP).astype(jnp.float32)
    weighted_rows = wo.reshape(N_TP, QUERY_WIDTH // N_TP, MODEL_WIDTH).astype(jnp.float32)
    term_list = jnp.einsum('vys,ysj->vyj', block_list, weighted_rows).astype(jnp.bfloat16)
    term_list = lax.optimization_barrier(term_list)
    branch = lax.optimization_barrier(jnp.sum(term_list.astype(jnp.float32), axis=1))
    return (xf + branch).astype(jnp.bfloat16)

def reference(hidden_entering, layer_norm_gain, query_matrix, output_matrix, adapter_down_weight, adapter_up_weight, key_value_cache, adapter_index, cached_lengths):
    hidden_state = hidden_entering
    collected = []
    for step_index in range(TICKS):
        groups = ((jnp.arange(SECTION_COUNT, dtype=jnp.int32) - step_index) % SECTION_COUNT).astype(jnp.int32)
        request_adapters = adapter_index[groups]
        request_lengths = cached_lengths[groups]
        layer_result = lax.map(layer_index, (hidden_state, layer_norm_gain, query_matrix, output_matrix, adapter_down_weight, adapter_up_weight, key_value_cache[:, step_index], request_adapters, request_lengths))
        collected.append(layer_result)
        hidden_state = jnp.roll(layer_result, 1, axis=0)
    return jnp.stack(collected, axis=1)
```

```python
import functools

import jax
import jax.numpy as jnp
from jax import lax
from jax.experimental import pallas as pl
from jax.experimental.pallas import tpu as pltpu
from jax.sharding import PartitionSpec as P

HD = 128
HEADS = 32
KVH = 4
ADAPTER_SCALE = 2.0
MESH = pl.DeviceIdType.MESH
BF16 = jnp.bfloat16
F32 = jnp.float32


def flipped(me, d):
    value, bit = me, 1
    while bit <= d:
        if d & bit:
            value = value + bit * (1 - 2 * ((me // bit) % 2))
        bit *= 2
    return value


def kernel(
    sections,
    parts,
    adapter_ref,
    lens_ref,
    x_ref,
    gain_ref,
    wq_hbm,
    wo_hbm,
    down_ref,
    up_ref,
    kv_hbm,
    out_ref,
    wq,
    wo,
    down32,
    kbuf,
    vbuf,
    xbuf,
    hbuf,
    ubuf,
    rbuf,
    sbuf,
    load_sem,
    kv_send,
    kv_recv,
    x_send,
    x_recv,
    u_send,
    u_recv,
    r_send,
    r_recv,
    z_send,
    z_recv,
):
    section = lax.axis_index("section")
    me = lax.axis_index("tp")
    ticks = kbuf.shape[0]
    rows, share = x_ref.shape[1], x_ref.shape[2]
    width = parts * share
    owned = kv_hbm.shape[2]
    context = kv_hbm.shape[3]
    feats = wq.shape[1]
    heads = feats // HD
    group = HEADS // KVH
    adapters, rank_share = down_ref.shape[1], down_ref.shape[2]
    rank_full = up_ref.shape[2]
    ranks = adapters * rank_share
    nxt = (section + 1) % sections
    prv = (section + sections - 1) % sections

    wq_copies = []
    for d in range(parts):
        lo = pl.multiple_of(flipped(me, d) * share, share)
        wq_copies.append(
            pltpu.make_async_copy(
                wq_hbm.at[0, pl.ds(lo, share), :], wq.at[pl.ds(lo, share), :], load_sem.at[d]
            )
        )
    wo_copy = pltpu.make_async_copy(wo_hbm.at[0], wo, load_sem.at[parts])
    for copy in wq_copies:
        copy.start()
    wo_copy.start()

    barrier = pltpu.get_barrier_semaphore()
    for d in range(1, parts):
        pl.semaphore_signal(
            barrier, inc=1, device_id=(section, flipped(me, d)), device_id_type=MESH
        )
    pl.semaphore_signal(barrier, inc=1, device_id=(nxt, me), device_id_type=MESH)
    pl.semaphore_signal(barrier, inc=1, device_id=(prv, me), device_id_type=MESH)
    for a in range(adapters):
        down32[a * rank_share : (a + 1) * rank_share, :] = down_ref[0, a].astype(F32)
    xbuf[0, 0] = x_ref[0]
    pl.semaphore_wait(barrier, parts + 1)

    def send(src, dst, ssem, rsem, device):
        copy = pltpu.make_async_remote_copy(
            src_ref=src,
            dst_ref=dst,
            send_sem=ssem,
            recv_sem=rsem,
            device_id=device,
            device_id_type=MESH,
        )
        copy.start()
        return copy

    far_first = list(range(parts - 1, 0, -1))
    pending = []

    def spread_x(t, src):
        copies = [None] * parts
        for d in far_first:
            copies[d] = send(
                src, xbuf.at[t, d], x_send.at[t, d], x_recv.at[t, d], (section, flipped(me, d))
            )
        pending.extend(c for c in copies if c is not None)
        return copies

    x_copies = spread_x(0, x_ref.at[0])

    def kv_head(device):
        return (device * heads) // group

    mine = pl.ds(pl.multiple_of(me * owned, owned), owned)
    kv_copies = []
    for d in [0] + far_first:
        peer = flipped(me, d)
        kcol = pl.multiple_of(kv_head(peer) * HD, HD)
        vcol = pl.multiple_of(KVH * HD + kv_head(peer) * HD, HD)
        for i, (col, buf) in enumerate(((kcol, kbuf), (vcol, vbuf))):
            src = kv_hbm.at[0, :, :, :, pl.ds(col, HD)]
            dst = buf.at[:, mine]
            if d == 0:
                copy = pltpu.make_async_copy(src, dst, kv_recv.at[i, 0])
                copy.start()
            else:
                copy = send(src, dst, kv_send.at[i, d], kv_recv.at[i, d], (section, peer))
                pending.append(copy)
            kv_copies.append((d, copy))

    row = lax.broadcasted_iota(jnp.int32, (ranks, adapters * rank_full), 0)
    col = lax.broadcasted_iota(jnp.int32, (ranks, adapters * rank_full), 1)
    place = jnp.where(
        col == (row // rank_share) * rank_full + me * rank_share + row % rank_share, 1.0, 0.0
    ).astype(BF16)

    for t in range(ticks):
        gidx = (section + sections - t) % sections
        r_id = lax.broadcasted_iota(jnp.int32, (rows, ranks), 0)
        a_id = lax.broadcasted_iota(jnp.int32, (rows, ranks), 1) // rank_share
        chosen = jnp.zeros((rows, ranks), jnp.int32)
        c_id = lax.broadcasted_iota(jnp.int32, (1, rows * context), 1)
        lens = jnp.zeros((1, rows * context), jnp.int32)
        for r in range(rows):
            chosen = jnp.where(r_id == r, adapter_ref[gidx, r], chosen)
            lens = jnp.where(c_id // context == r, lens_ref[gidx, r], lens)
        onehot = jnp.where(chosen == a_id, 1.0, 0.0)
        m_row = lax.broadcasted_iota(jnp.int32, (heads * rows, rows * context), 0) % rows
        m_col = lax.broadcasted_iota(jnp.int32, (heads * rows, rows * context), 1)
        valid = (m_row == m_col // context) & (m_col % context < lens)

        if t > 0:
            z_copy.wait()
            x_copies = spread_x(t, xbuf.at[t, 0])

        squares = jnp.zeros((rows, 1), F32)
        acc_u = jnp.zeros((rows, ranks), F32)
        acc_q = jnp.zeros((rows, feats), F32)
        for d in range(parts):
            if d > 0:
                x_copies[d].wait_recv()
            lo = pl.multiple_of(flipped(me, d) * share, share)
            xf = xbuf[t, d].astype(F32)
            squares += jnp.sum(xf * xf, axis=-1, keepdims=True)
            h = (xf * gain_ref[:, pl.ds(lo, share)].astype(F32)).astype(BF16)
            hbuf[d] = h
            acc_u += lax.dot_general(
                h,
                down32[:, pl.ds(lo, share)].astype(BF16),
                (((1,), (1,)), ((), ())),
                preferred_element_type=F32,
            )
            if d < parts // 2:
                if t == 0:
                    wq_copies[d].wait()
                acc_q += jnp.dot(h, wq[pl.ds(lo, share), :], preferred_element_type=F32)
        inv = lax.rsqrt(squares * (1.0 / width) + 1e-05)
        u_own = (acc_u * inv * onehot).astype(BF16)
        u_placed = jnp.dot(u_own, place, preferred_element_type=F32)
        ubuf[t, 0] = u_placed.astype(BF16)
        u_copies = [None] * parts
        for d in far_first:
            u_copies[d] = send(
                ubuf.at[t, 0],
                ubuf.at[t, d],
                u_send.at[t, d],
                u_recv.at[t, d],
                (section, flipped(me, d)),
            )
            pending.append(u_copies[d])
        for d in range(parts // 2, parts):
            lo = pl.multiple_of(flipped(me, d) * share, share)
            if t == 0:
                wq_copies[d].wait()
            acc_q += jnp.dot(hbuf[d], wq[pl.ds(lo, share), :], preferred_element_type=F32)
        u_sum = u_placed
        for d in range(1, parts):
            u_copies[d].wait_recv()
            u_sum += ubuf[t, d].astype(F32)
        up = up_ref[0].reshape(adapters * rank_full, feats)
        delta = jnp.dot(u_sum.astype(BF16), up, preferred_element_type=F32)
        query = (acc_q * inv + ADAPTER_SCALE * delta).astype(BF16)

        if t == 0:
            for d, copy in kv_copies:
                if d == 0:
                    copy.wait()
                else:
                    copy.wait_recv()
        qh = jnp.concatenate([query[:, i * HD : (i + 1) * HD] for i in range(heads)], axis=0)
        keys = kbuf[t].reshape(rows * context, HD)
        values = vbuf[t].reshape(rows * context, HD)
        scores = lax.dot_general(
            qh, keys, (((1,), (1,)), ((), ())), preferred_element_type=F32
        ) * HD ** (-0.5)
        scores = jnp.where(valid, scores, -1e30)
        top = jnp.max(scores, axis=-1, keepdims=True)
        expo = jnp.where(valid, jnp.exp(scores - top), 0.0)
        weights = (expo / jnp.sum(expo, axis=-1, keepdims=True)).astype(BF16)
        attn = jnp.dot(weights, values, preferred_element_type=F32).astype(BF16)
        attn = jnp.concatenate([attn[i * rows : (i + 1) * rows] for i in range(heads)], axis=1)

        if t == 0:
            wo_copy.wait()
        r_copies = [None] * parts
        for d in far_first:
            peer = flipped(me, d)
            lo = pl.multiple_of(peer * share, share)
            sbuf[t, d] = jnp.dot(
                attn, wo[:, pl.ds(lo, share)], preferred_element_type=F32
            ).astype(BF16)
            r_copies[d] = send(
                sbuf.at[t, d], rbuf.at[t, d], r_send.at[t, d], r_recv.at[t, d], (section, peer)
            )
            pending.append(r_copies[d])
        lo = pl.multiple_of(me * share, share)
        total = (
            jnp.dot(attn, wo[:, pl.ds(lo, share)], preferred_element_type=F32)
            .astype(BF16)
            .astype(F32)
        )
        for d in range(1, parts):
            r_copies[d].wait_recv()
            total += rbuf[t, d].astype(F32)
        result = (xbuf[t, 0].astype(F32) + total).astype(BF16)
        out_ref[0, t] = result
        if t + 1 < ticks:
            z_copy = send(
                out_ref.at[0, t], xbuf.at[t + 1, 0], z_send.at[t], z_recv.at[t], (nxt, me)
            )

    for copy in pending:
        copy.wait_send()


def local(
    hidden_entering,
    layer_norm_gain,
    query_matrix,
    output_matrix,
    adapter_down_weight,
    adapter_up_weight,
    key_value_cache,
    adapter_index,
    cached_lengths,
):
    sections = lax.axis_size("section")
    parts = lax.axis_size("tp")
    rows, share = hidden_entering.shape[1:]
    ticks, _, context, _ = key_value_cache.shape[1:]
    width, feats = query_matrix.shape[1:]
    adapters, rank_share = adapter_down_weight.shape[1:3]
    rank_full = adapter_up_weight.shape[2]
    vmem = pl.BlockSpec(memory_space=pltpu.VMEM)
    smem = pl.BlockSpec(memory_space=pltpu.SMEM)
    hbm = pl.BlockSpec(memory_space=pl.ANY)
    dma = pltpu.SemaphoreType.DMA
    return pl.pallas_call(
        functools.partial(kernel, sections, parts),
        out_shape=jax.ShapeDtypeStruct((1, ticks, rows, share), BF16),
        in_specs=[smem, smem, vmem, vmem, hbm, hbm, vmem, vmem, hbm],
        out_specs=vmem,
        scratch_shapes=[
            pltpu.VMEM((width, feats), BF16),
            pltpu.VMEM((feats, width), BF16),
            pltpu.VMEM((adapters * rank_share, width), F32),
            pltpu.VMEM((ticks, rows, context, HD), BF16),
            pltpu.VMEM((ticks, rows, context, HD), BF16),
            pltpu.VMEM((ticks, parts, rows, share), BF16),
            pltpu.VMEM((parts, rows, share), BF16),
            pltpu.VMEM((ticks, parts, rows, adapters * rank_full), BF16),
            pltpu.VMEM((ticks, parts, rows, share), BF16),
            pltpu.VMEM((ticks, parts, rows, share), BF16),
            dma((parts + 1,)),
            dma((2, parts)),
            dma((2, parts)),
            dma((ticks, parts)),
            dma((ticks, parts)),
            dma((ticks, parts)),
            dma((ticks, parts)),
            dma((ticks, parts)),
            dma((ticks, parts)),
            dma((ticks,)),
            dma((ticks,)),
        ],
        compiler_params=pltpu.CompilerParams(
            collective_id=0, has_side_effects=True, vmem_limit_bytes=56 << 20
        ),
    )(
        adapter_index,
        cached_lengths,
        hidden_entering,
        layer_norm_gain,
        query_matrix,
        output_matrix,
        adapter_down_weight,
        adapter_up_weight,
        key_value_cache,
    )


def solution(mesh):
    placed = (
        P("section", None, "tp"),
        P("section", None),
        P("section", None, "tp"),
        P("section", "tp", None),
        P("section", None, "tp", None),
        P("section", None, None, "tp"),
        P("section", None, "tp", None, None),
        P(),
        P(),
    )
    return jax.shard_map(
        local, mesh=mesh, in_specs=placed, out_specs=P("section", None, None, "tp"), check_vma=False
    )
```

```python
import functools

import jax
import jax.numpy as jnp
from jax import lax
from jax.experimental import pallas as pl
from jax.experimental.pallas import tpu as pltpu
from jax.sharding import PartitionSpec as P

HD = 128
HEADS = 32
KVH = 4
ADAPTER_SCALE = 2.0
MESH = pl.DeviceIdType.MESH
BF16 = jnp.bfloat16
F32 = jnp.float32


def flipped(me, d):
    value, bit = me, 1
    while bit <= d:
        if d & bit:
            value = value + bit * (1 - 2 * ((me // bit) % 2))
        bit *= 2
    return value


def kernel(
    sections,
    parts,
    adapter_ref,
    lens_ref,
    x_ref,
    gain_ref,
    wq_hbm,
    wo_hbm,
    down_ref,
    up_ref,
    kv_hbm,
    out_ref,
    wq,
    wo,
    down32,
    dparts,
    dcols32,
    dcols,
    upbuf,
    kbuf,
    vbuf,
    xbuf,
    hbuf,
    ubuf,
    rbuf,
    sbuf,
    load_sem,
    d_send,
    d_recv,
    kv_send,
    kv_recv,
    x_send,
    x_recv,
    u_send,
    u_recv,
    r_send,
    r_recv,
    z_send,
    z_recv,
):
    section = lax.axis_index("section")
    me = lax.axis_index("tp")
    ticks = kbuf.shape[0]
    rows, share = x_ref.shape[1], x_ref.shape[2]
    width = parts * share
    owned = kv_hbm.shape[2]
    context = kv_hbm.shape[3]
    feats = wq.shape[1]
    heads = feats // HD
    group = HEADS // KVH
    adapters, rank_share = down_ref.shape[1], down_ref.shape[2]
    rank_full = up_ref.shape[2]
    ranks = adapters * rank_share
    nxt = (section + 1) % sections
    prv = (section + sections - 1) % sections

    wq_copies = []
    for d in range(parts):
        lo = pl.multiple_of(flipped(me, d) * share, share)
        wq_copies.append(
            pltpu.make_async_copy(
                wq_hbm.at[0, pl.ds(lo, share), :], wq.at[pl.ds(lo, share), :], load_sem.at[d]
            )
        )
    wo_copy = pltpu.make_async_copy(wo_hbm.at[0], wo, load_sem.at[parts])
    for copy in wq_copies:
        copy.start()
    wo_copy.start()

    barrier = pltpu.get_barrier_semaphore()
    for d in range(1, parts):
        pl.semaphore_signal(
            barrier, inc=1, device_id=(section, flipped(me, d)), device_id_type=MESH
        )
    pl.semaphore_signal(barrier, inc=1, device_id=(nxt, me), device_id_type=MESH)
    pl.semaphore_signal(barrier, inc=1, device_id=(prv, me), device_id_type=MESH)
    for a in range(adapters):
        down32[a * rank_share : (a + 1) * rank_share, :] = down_ref[0, a].astype(F32)
    xbuf[0, 0] = x_ref[0]
    pl.semaphore_wait(barrier, parts + 1)

    def send(src, dst, ssem, rsem, device):
        copy = pltpu.make_async_remote_copy(
            src_ref=src,
            dst_ref=dst,
            send_sem=ssem,
            recv_sem=rsem,
            device_id=device,
            device_id_type=MESH,
        )
        copy.start()
        return copy

    far_first = list(range(parts - 1, 0, -1))
    pending = []

    def spread_x(t, src):
        copies = [None] * parts
        for d in far_first:
            copies[d] = send(
                src, xbuf.at[t, d], x_send.at[t, d], x_recv.at[t, d], (section, flipped(me, d))
            )
        pending.extend(c for c in copies if c is not None)
        return copies

    def spread_u(t):
        copies = [None] * parts
        for d in far_first:
            copies[d] = send(
                ubuf.at[t, 0],
                ubuf.at[t, d],
                u_send.at[t, d],
                u_recv.at[t, d],
                (section, flipped(me, d)),
            )
            pending.append(copies[d])
        return copies

    x_copies = spread_x(0, x_ref.at[0])

    def kv_head(device):
        return (device * heads) // group

    def rows_of(device):
        return pl.ds(pl.multiple_of(device * owned, owned), owned)

    partner = flipped(me, 1)
    kv_copies = {}

    def send_cache(t):
        for d in [0] + [e for e in far_first if e % 2 == 0] + [1]:
            peer = flipped(me, d)
            for i, buf in enumerate((kbuf, vbuf)):
                col = pl.multiple_of(i * KVH * HD + kv_head(peer) * HD, HD)
                src = kv_hbm.at[0, t, :, :, pl.ds(col, HD)]
                dst = buf.at[t, rows_of(me)]
                if d == 0:
                    copy = pltpu.make_async_copy(src, dst, kv_recv.at[t, i, 0])
                    copy.start()
                else:
                    copy = send(
                        src, dst, kv_send.at[t, i, d], kv_recv.at[t, i, d], (section, peer)
                    )
                    pending.append(copy)
                kv_copies[t, i, d] = copy

    def forward_cache(t):
        for d in range(2, parts, 2):
            for i, buf in enumerate((kbuf, vbuf)):
                kv_copies[t, i, d].wait_recv()
                block = buf.at[t, rows_of(flipped(me, d))]
                copy = send(
                    block,
                    block,
                    kv_send.at[t, i, d + 1],
                    kv_recv.at[t, i, d + 1],
                    (section, partner),
                )
                pending.append(copy)
                kv_copies[t, i, d + 1] = copy

    def wait_cache(t):
        for i in range(2):
            kv_copies[t, i, 0].wait()
            for d in range(1, parts):
                if d == 1 or d % 2 == 1:
                    kv_copies[t, i, d].wait_recv()

    d_copies = {}

    def send_down(peers):
        for d in peers:
            peer = flipped(me, d)
            lo = pl.multiple_of(peer * share, share)
            d_copies[d] = send(
                down_ref.at[0, :, :, pl.ds(lo, share)],
                dparts.at[me],
                d_send.at[d],
                d_recv.at[d],
                (section, peer),
            )
            pending.append(d_copies[d])

    down_first = [d for d in far_first if d >= parts - parts // 4 or d == 1]
    down_later = [d for d in far_first if d not in down_first]
    send_cache(0)
    my_cols = pl.ds(pl.multiple_of(me * share, share), share)
    dparts[me] = down_ref[0, :, :, my_cols]
    send_down(down_first)

    row = lax.broadcasted_iota(jnp.int32, (ranks, adapters * rank_full), 0)
    col = lax.broadcasted_iota(jnp.int32, (ranks, adapters * rank_full), 1)
    place = jnp.where(col == me * ranks + row, 1.0, 0.0).astype(BF16)
    full = adapters * rank_full
    row = lax.broadcasted_iota(jnp.int32, (full, full), 0)
    col = lax.broadcasted_iota(jnp.int32, (full, full), 1)
    source = (
        (row // rank_share) % adapters * rank_full + row // ranks * rank_share + row % rank_share
    )
    order = jnp.where(col == source, 1.0, 0.0).astype(BF16)
    up = jnp.dot(order, up_ref[0].reshape(full, feats), preferred_element_type=F32).astype(BF16)
    upbuf[...] = up

    for t in range(ticks):
        gidx = (section + sections - t) % sections
        r_id = lax.broadcasted_iota(jnp.int32, (rows, full), 0)
        a_id = lax.broadcasted_iota(jnp.int32, (rows, full), 1) // rank_share % adapters
        chosen = jnp.zeros((rows, full), jnp.int32)
        c_id = lax.broadcasted_iota(jnp.int32, (1, rows * context), 1)
        lens = jnp.zeros((1, rows * context), jnp.int32)
        for r in range(rows):
            chosen = jnp.where(r_id == r, adapter_ref[gidx, r], chosen)
            lens = jnp.where(c_id // context == r, lens_ref[gidx, r], lens)
        onehot = jnp.where(chosen == a_id, 1.0, 0.0)
        m_row = lax.broadcasted_iota(jnp.int32, (heads * rows, rows * context), 0) % rows
        m_col = lax.broadcasted_iota(jnp.int32, (heads * rows, rows * context), 1)
        valid = (m_row == m_col // context) & (m_col % context < lens)

        if t > 0:
            z_copy.wait_recv()
            x_copies = spread_x(t, xbuf.at[t, 0])
            h = (xbuf[t, 0].astype(F32) * gain_ref[:, my_cols].astype(F32)).astype(BF16)
            u_part = lax.dot_general(
                h, dcols[...], (((1,), (1,)), ((), ())), preferred_element_type=F32
            )
            ubuf[t, 0] = u_part.astype(BF16)
            u_copies = spread_u(t)

        squares = jnp.zeros((rows, 1), F32)
        acc_u = jnp.zeros((rows, ranks), F32)
        acc_q = jnp.zeros((rows, feats), F32)
        for d in range(parts):
            if d > 0:
                x_copies[d].wait_recv()
            lo = pl.multiple_of(flipped(me, d) * share, share)
            xf = xbuf[t, d].astype(F32)
            squares += jnp.sum(xf * xf, axis=-1, keepdims=True)
            h = (xf * gain_ref[:, pl.ds(lo, share)].astype(F32)).astype(BF16)
            if t == 0:
                hbuf[d] = h
                acc_u += lax.dot_general(
                    h,
                    down32[:, pl.ds(lo, share)].astype(BF16),
                    (((1,), (1,)), ((), ())),
                    preferred_element_type=F32,
                )
            if t > 0 or d < parts // 2:
                if t == 0:
                    wq_copies[d].wait()
                acc_q += jnp.dot(h, wq[pl.ds(lo, share), :], preferred_element_type=F32)
        inv = lax.rsqrt(squares * (1.0 / width) + 1e-05)
        if t == 0:
            u_own = (acc_u * inv).astype(BF16)
            u_sum = jnp.dot(u_own, place, preferred_element_type=F32)
            ubuf[t, 0] = u_sum.astype(BF16)
            u_copies = spread_u(t)
            send_down(down_later)
            for d in range(parts // 2, parts):
                lo = pl.multiple_of(flipped(me, d) * share, share)
                wq_copies[d].wait()
                acc_q += jnp.dot(hbuf[d], wq[pl.ds(lo, share), :], preferred_element_type=F32)
        else:
            u_sum = u_part
        forward_cache(t)
        for d in range(1, parts):
            u_copies[d].wait_recv()
            u_sum += ubuf[t, d].astype(F32)
        if t > 0:
            u_sum = u_sum * inv
        u_sum = (u_sum * onehot).astype(BF16)
        delta = jnp.dot(u_sum, upbuf[...], preferred_element_type=F32)
        query = (acc_q * inv + ADAPTER_SCALE * delta).astype(BF16)

        wait_cache(t)
        qh = jnp.concatenate([query[:, i * HD : (i + 1) * HD] for i in range(heads)], axis=0)
        keys = kbuf[t].reshape(rows * context, HD)
        values = vbuf[t].reshape(rows * context, HD)
        scores = lax.dot_general(
            qh, keys, (((1,), (1,)), ((), ())), preferred_element_type=F32
        ) * HD ** (-0.5)
        scores = jnp.where(valid, scores, -1e30)
        top = jnp.max(scores, axis=-1, keepdims=True)
        expo = jnp.where(valid, jnp.exp(scores - top), 0.0)
        weights = (expo / jnp.sum(expo, axis=-1, keepdims=True)).astype(BF16)
        attn = jnp.dot(weights, values, preferred_element_type=F32).astype(BF16)
        attn = jnp.concatenate([attn[i * rows : (i + 1) * rows] for i in range(heads)], axis=1)

        if t == 0:
            wo_copy.wait()
        r_copies = [None] * parts
        for d in far_first:
            peer = flipped(me, d)
            lo = pl.multiple_of(peer * share, share)
            sbuf[t, d] = jnp.dot(
                attn, wo[:, pl.ds(lo, share)], preferred_element_type=F32
            ).astype(BF16)
            r_copies[d] = send(
                sbuf.at[t, d], rbuf.at[t, d], r_send.at[t, d], r_recv.at[t, d], (section, peer)
            )
            pending.append(r_copies[d])
        if t + 1 < ticks:
            send_cache(t + 1)
        total = (
            jnp.dot(attn, wo[:, my_cols], preferred_element_type=F32)
            .astype(BF16)
            .astype(F32)
        )
        if t == 0:
            for d in range(1, parts):
                d_copies[d].wait_recv()
            for p in range(parts):
                for a in range(adapters):
                    lo = p * ranks + a * rank_share
                    dcols32[lo : lo + rank_share, :] = dparts[p, a].astype(F32)
            dcols[...] = dcols32[...].astype(BF16)
        for d in range(1, parts):
            r_copies[d].wait_recv()
            total += rbuf[t, d].astype(F32)
        result = (xbuf[t, 0].astype(F32) + total).astype(BF16)
        out_ref[0, t] = result
        if t + 1 < ticks:
            z_copy = send(
                out_ref.at[0, t], xbuf.at[t + 1, 0], z_send.at[t], z_recv.at[t], (nxt, me)
            )
            pending.append(z_copy)

    for copy in pending:
        copy.wait_send()


def local(
    hidden_entering,
    layer_norm_gain,
    query_matrix,
    output_matrix,
    adapter_down_weight,
    adapter_up_weight,
    key_value_cache,
    adapter_index,
    cached_lengths,
):
    sections = lax.axis_size("section")
    parts = lax.axis_size("tp")
    rows, share = hidden_entering.shape[1:]
    ticks, _, context, _ = key_value_cache.shape[1:]
    width, feats = query_matrix.shape[1:]
    adapters, rank_share = adapter_down_weight.shape[1:3]
    rank_full = adapter_up_weight.shape[2]
    vmem = pl.BlockSpec(memory_space=pltpu.VMEM)
    smem = pl.BlockSpec(memory_space=pltpu.SMEM)
    hbm = pl.BlockSpec(memory_space=pl.ANY)
    dma = pltpu.SemaphoreType.DMA
    return pl.pallas_call(
        functools.partial(kernel, sections, parts),
        out_shape=jax.ShapeDtypeStruct((1, ticks, rows, share), BF16),
        in_specs=[smem, smem, vmem, vmem, hbm, hbm, vmem, vmem, hbm],
        out_specs=vmem,
        scratch_shapes=[
            pltpu.VMEM((width, feats), BF16),
            pltpu.VMEM((feats, width), BF16),
            pltpu.VMEM((adapters * rank_share, width), F32),
            pltpu.VMEM((parts, adapters, rank_share, share), BF16),
            pltpu.VMEM((adapters * rank_full, share), F32),
            pltpu.VMEM((adapters * rank_full, share), BF16),
            pltpu.VMEM((adapters * rank_full, feats), BF16),
            pltpu.VMEM((ticks, rows, context, HD), BF16),
            pltpu.VMEM((ticks, rows, context, HD), BF16),
            pltpu.VMEM((ticks, parts, rows, share), BF16),
            pltpu.VMEM((parts, rows, share), BF16),
            pltpu.VMEM((ticks, parts, rows, adapters * rank_full), BF16),
            pltpu.VMEM((ticks, parts, rows, share), BF16),
            pltpu.VMEM((ticks, parts, rows, share), BF16),
            dma((parts + 1,)),
            dma((parts,)),
            dma((parts,)),
            dma((ticks, 2, parts)),
            dma((ticks, 2, parts)),
            dma((ticks, parts)),
            dma((ticks, parts)),
            dma((ticks, parts)),
            dma((ticks, parts)),
            dma((ticks, parts)),
            dma((ticks, parts)),
            dma((ticks,)),
            dma((ticks,)),
        ],
        compiler_params=pltpu.CompilerParams(
            collective_id=0, has_side_effects=True, vmem_limit_bytes=56 << 20
        ),
    )(
        adapter_index,
        cached_lengths,
        hidden_entering,
        layer_norm_gain,
        query_matrix,
        output_matrix,
        adapter_down_weight,
        adapter_up_weight,
        key_value_cache,
    )


def solution(mesh):
    placed = (
        P("section", None, "tp"),
        P("section", None),
        P("section", None, "tp"),
        P("section", "tp", None),
        P("section", None, "tp", None),
        P("section", None, None, "tp"),
        P("section", None, "tp", None, None),
        P(),
        P(),
    )
    return jax.shard_map(
        local, mesh=mesh, in_specs=placed, out_specs=P("section", None, None, "tp"), check_vma=False
    )
```

```python
import functools

import jax
import jax.numpy as jnp
from jax import lax
from jax.experimental import pallas as pl
from jax.experimental.pallas import tpu as pltpu
from jax.sharding import PartitionSpec as P

HD = 128
HEADS = 32
KVH = 4
ADAPTER_SCALE = 2.0
MESH = pl.DeviceIdType.MESH
BF16 = jnp.bfloat16
F32 = jnp.float32


def flipped(me, d):
    value, bit = me, 1
    while bit <= d:
        if d & bit:
            value = value + bit * (1 - 2 * ((me // bit) % 2))
        bit *= 2
    return value


def kernel(
    sections,
    parts,
    adapter_ref,
    lens_ref,
    x_ref,
    gain_ref,
    wq_hbm,
    wo_hbm,
    down_ref,
    up_ref,
    kv_hbm,
    out_ref,
    wq,
    wo,
    down32,
    dparts,
    dcols32,
    dcols,
    upbuf,
    kbuf,
    vbuf,
    xbuf,
    hbuf,
    ubuf,
    rbuf,
    sbuf,
    load_sem,
    d_send,
    d_recv,
    kv_send,
    kv_recv,
    x_send,
    x_recv,
    u_send,
    u_recv,
    r_send,
    r_recv,
    z_send,
    z_recv,
):
    section = lax.axis_index("section")
    me = lax.axis_index("tp")
    ticks = kbuf.shape[0]
    rows, share = x_ref.shape[1], x_ref.shape[2]
    width = parts * share
    owned = kv_hbm.shape[2]
    context = kv_hbm.shape[3]
    feats = wq.shape[1]
    heads = feats // HD
    group = HEADS // KVH
    adapters, rank_share = down_ref.shape[1], down_ref.shape[2]
    rank_full = up_ref.shape[2]
    ranks = adapters * rank_share
    nxt = (section + 1) % sections
    prv = (section + sections - 1) % sections

    wq_copies = []
    for d in range(parts):
        lo = pl.multiple_of(flipped(me, d) * share, share)
        wq_copies.append(
            pltpu.make_async_copy(
                wq_hbm.at[0, pl.ds(lo, share), :], wq.at[pl.ds(lo, share), :], load_sem.at[d]
            )
        )
    wo_copy = pltpu.make_async_copy(wo_hbm.at[0], wo, load_sem.at[parts])
    for copy in wq_copies:
        copy.start()
    wo_copy.start()

    barrier = pltpu.get_barrier_semaphore()
    for d in range(1, parts):
        pl.semaphore_signal(
            barrier, inc=1, device_id=(section, flipped(me, d)), device_id_type=MESH
        )
    pl.semaphore_signal(barrier, inc=1, device_id=(nxt, me), device_id_type=MESH)
    pl.semaphore_signal(barrier, inc=1, device_id=(prv, me), device_id_type=MESH)
    for a in range(adapters):
        down32[a * rank_share : (a + 1) * rank_share, :] = down_ref[0, a].astype(F32)
    xbuf[0, 0] = x_ref[0]
    pl.semaphore_wait(barrier, parts + 1)

    def send(src, dst, ssem, rsem, device):
        copy = pltpu.make_async_remote_copy(
            src_ref=src,
            dst_ref=dst,
            send_sem=ssem,
            recv_sem=rsem,
            device_id=device,
            device_id_type=MESH,
        )
        copy.start()
        return copy

    far_first = list(range(parts - 1, 0, -1))
    relayed = [d for d in range(2, parts, 2) if d >= parts - parts // 4]
    via_partner = [d + 1 for d in relayed]
    direct = [d for d in far_first if d not in via_partner]
    near = [d for d in range(2, parts) if d not in relayed and d not in via_partner]
    near = [d for d in near if d % 2 == 0] + [d for d in near if d % 2 == 1]
    arrival = [0, 1] + relayed + near + via_partner
    partner = flipped(me, 1)
    pending = []

    def spread_x(t, src):
        copies = [None] * parts
        for d in direct:
            copies[d] = send(
                src, xbuf.at[t, d], x_send.at[t, d], x_recv.at[t, d], (section, flipped(me, d))
            )
        pending.extend(c for c in copies if c is not None)
        return copies

    def spread_u(t):
        copies = [None] * parts
        for d in far_first:
            copies[d] = send(
                ubuf.at[t, 0],
                ubuf.at[t, d],
                u_send.at[t, d],
                u_recv.at[t, d],
                (section, flipped(me, d)),
            )
            pending.append(copies[d])
        return copies

    x_copies = spread_x(0, x_ref.at[0])

    def kv_head(device):
        return (device * heads) // group

    def rows_of(device):
        return pl.ds(pl.multiple_of(device * owned, owned), owned)

    kv_copies = {}

    def send_cache(t):
        for d in [0] + [e for e in far_first if e % 2 == 0] + [1]:
            peer = flipped(me, d)
            for i, buf in enumerate((kbuf, vbuf)):
                col = pl.multiple_of(i * KVH * HD + kv_head(peer) * HD, HD)
                src = kv_hbm.at[0, t, :, :, pl.ds(col, HD)]
                dst = buf.at[t, rows_of(me)]
                if d == 0:
                    copy = pltpu.make_async_copy(src, dst, kv_recv.at[t, i, 0])
                    copy.start()
                else:
                    copy = send(
                        src, dst, kv_send.at[t, i, d], kv_recv.at[t, i, d], (section, peer)
                    )
                    pending.append(copy)
                kv_copies[t, i, d] = copy

    def forward_cache(t):
        for d in range(2, parts, 2):
            for i, buf in enumerate((kbuf, vbuf)):
                kv_copies[t, i, d].wait_recv()
                block = buf.at[t, rows_of(flipped(me, d))]
                copy = send(
                    block,
                    block,
                    kv_send.at[t, i, d + 1],
                    kv_recv.at[t, i, d + 1],
                    (section, partner),
                )
                pending.append(copy)
                kv_copies[t, i, d + 1] = copy

    def wait_cache(t):
        for i in range(2):
            kv_copies[t, i, 0].wait()
            for d in range(1, parts):
                if d == 1 or d % 2 == 1:
                    kv_copies[t, i, d].wait_recv()

    d_copies = {}

    def send_down(peers):
        for d in peers:
            peer = flipped(me, d)
            lo = pl.multiple_of(peer * share, share)
            d_copies[d] = send(
                down_ref.at[0, :, :, pl.ds(lo, share)],
                dparts.at[me],
                d_send.at[d],
                d_recv.at[d],
                (section, peer),
            )
            pending.append(d_copies[d])

    down_first = [d for d in far_first if d >= parts - parts // 4 or d == 1]
    down_later = [d for d in far_first if d not in down_first]
    send_cache(0)
    my_cols = pl.ds(pl.multiple_of(me * share, share), share)
    dparts[me] = down_ref[0, :, :, my_cols]
    send_down(down_first)

    row = lax.broadcasted_iota(jnp.int32, (ranks, adapters * rank_full), 0)
    col = lax.broadcasted_iota(jnp.int32, (ranks, adapters * rank_full), 1)
    place = jnp.where(col == me * ranks + row, 1.0, 0.0).astype(BF16)
    full = adapters * rank_full
    row = lax.broadcasted_iota(jnp.int32, (full, full), 0)
    col = lax.broadcasted_iota(jnp.int32, (full, full), 1)
    source = (
        (row // rank_share) % adapters * rank_full + row // ranks * rank_share + row % rank_share
    )
    order = jnp.where(col == source, 1.0, 0.0).astype(BF16)
    up = jnp.dot(order, up_ref[0].reshape(full, feats), preferred_element_type=F32).astype(BF16)
    upbuf[...] = up

    for t in range(ticks):
        gidx = (section + sections - t) % sections
        r_id = lax.broadcasted_iota(jnp.int32, (rows, full), 0)
        a_id = lax.broadcasted_iota(jnp.int32, (rows, full), 1) // rank_share % adapters
        chosen = jnp.zeros((rows, full), jnp.int32)
        c_id = lax.broadcasted_iota(jnp.int32, (1, rows * context), 1)
        lens = jnp.zeros((1, rows * context), jnp.int32)
        for r in range(rows):
            chosen = jnp.where(r_id == r, adapter_ref[gidx, r], chosen)
            lens = jnp.where(c_id // context == r, lens_ref[gidx, r], lens)
        onehot = jnp.where(chosen == a_id, 1.0, 0.0)
        m_row = lax.broadcasted_iota(jnp.int32, (heads * rows, rows * context), 0) % rows
        m_col = lax.broadcasted_iota(jnp.int32, (heads * rows, rows * context), 1)
        valid = (m_row == m_col // context) & (m_col % context < lens)

        if t > 0:
            z_copy.wait_recv()
            x_copies = spread_x(t, xbuf.at[t, 0])
            h = (xbuf[t, 0].astype(F32) * gain_ref[:, my_cols].astype(F32)).astype(BF16)
            u_part = lax.dot_general(
                h, dcols[...], (((1,), (1,)), ((), ())), preferred_element_type=F32
            )
            ubuf[t, 0] = u_part.astype(BF16)
            u_copies = spread_u(t)

        squares = jnp.zeros((rows, 1), F32)
        acc_u = jnp.zeros((rows, ranks), F32)
        acc_q = jnp.zeros((rows, feats), F32)
        for k, d in enumerate(arrival):
            if d > 0:
                x_copies[d].wait_recv()
            if d in relayed:
                x_copies[d + 1] = send(
                    xbuf.at[t, d],
                    xbuf.at[t, d + 1],
                    x_send.at[t, d + 1],
                    x_recv.at[t, d + 1],
                    (section, partner),
                )
                pending.append(x_copies[d + 1])
            lo = pl.multiple_of(flipped(me, d) * share, share)
            xf = xbuf[t, d].astype(F32)
            squares += jnp.sum(xf * xf, axis=-1, keepdims=True)
            h = (xf * gain_ref[:, pl.ds(lo, share)].astype(F32)).astype(BF16)
            if t == 0:
                hbuf[d] = h
                acc_u += lax.dot_general(
                    h,
                    down32[:, pl.ds(lo, share)].astype(BF16),
                    (((1,), (1,)), ((), ())),
                    preferred_element_type=F32,
                )
            if t > 0 or k < parts // 2:
                if t == 0:
                    wq_copies[d].wait()
                acc_q += jnp.dot(h, wq[pl.ds(lo, share), :], preferred_element_type=F32)
        inv = lax.rsqrt(squares * (1.0 / width) + 1e-05)
        if t == 0:
            u_own = (acc_u * inv).astype(BF16)
            u_sum = jnp.dot(u_own, place, preferred_element_type=F32)
            ubuf[t, 0] = u_sum.astype(BF16)
            u_copies = spread_u(t)
            send_down(down_later)
            for d in arrival[parts // 2 :]:
                lo = pl.multiple_of(flipped(me, d) * share, share)
                wq_copies[d].wait()
                acc_q += jnp.dot(hbuf[d], wq[pl.ds(lo, share), :], preferred_element_type=F32)
        else:
            u_sum = u_part
        forward_cache(t)
        for d in range(1, parts):
            u_copies[d].wait_recv()
            u_sum += ubuf[t, d].astype(F32)
        if t > 0:
            u_sum = u_sum * inv
        u_sum = (u_sum * onehot).astype(BF16)
        delta = jnp.dot(u_sum, upbuf[...], preferred_element_type=F32)
        query = (acc_q * inv + ADAPTER_SCALE * delta).astype(BF16)

        wait_cache(t)
        qh = jnp.concatenate([query[:, i * HD : (i + 1) * HD] for i in range(heads)], axis=0)
        keys = kbuf[t].reshape(rows * context, HD)
        values = vbuf[t].reshape(rows * context, HD)
        scores = lax.dot_general(
            qh, keys, (((1,), (1,)), ((), ())), preferred_element_type=F32
        ) * HD ** (-0.5)
        scores = jnp.where(valid, scores, -1e30)
        top = jnp.max(scores, axis=-1, keepdims=True)
        expo = jnp.where(valid, jnp.exp(scores - top), 0.0)
        weights = (expo / jnp.sum(expo, axis=-1, keepdims=True)).astype(BF16)
        attn = jnp.dot(weights, values, preferred_element_type=F32).astype(BF16)
        attn = jnp.concatenate([attn[i * rows : (i + 1) * rows] for i in range(heads)], axis=1)

        if t == 0:
            wo_copy.wait()
        r_copies = [None] * parts

        def term(d):
            lo = pl.multiple_of(flipped(me, d) * share, share)
            return jnp.dot(attn, wo[:, pl.ds(lo, share)], preferred_element_type=F32).astype(BF16)

        def send_term(d, slot, device):
            r_copies[slot] = send(
                sbuf.at[t, d],
                rbuf.at[t, slot],
                r_send.at[t, slot],
                r_recv.at[t, slot],
                (section, device),
            )
            pending.append(r_copies[slot])

        for d in via_partner:
            sbuf[t, d] = term(d)
            send_term(d, d, partner)
        for d in near:
            sbuf[t, d] = term(d)
            send_term(d, d, flipped(me, d))
        for d in relayed:
            pair = term(d).astype(F32)
            r_copies[d + 1].wait_recv()
            sbuf[t, d] = (pair + rbuf[t, d + 1].astype(F32)).astype(BF16)
            send_term(d, d, flipped(me, d))
        sbuf[t, 1] = term(1)
        send_term(1, 1, partner)
        if t + 1 < ticks:
            send_cache(t + 1)
        total = (
            jnp.dot(attn, wo[:, my_cols], preferred_element_type=F32)
            .astype(BF16)
            .astype(F32)
        )
        if t == 0:
            for d in range(1, parts):
                d_copies[d].wait_recv()
            for p in range(parts):
                for a in range(adapters):
                    lo = p * ranks + a * rank_share
                    dcols32[lo : lo + rank_share, :] = dparts[p, a].astype(F32)
            dcols[...] = dcols32[...].astype(BF16)
        for d in [1] + near + relayed:
            r_copies[d].wait_recv()
            total += rbuf[t, d].astype(F32)
        result = (xbuf[t, 0].astype(F32) + total).astype(BF16)
        out_ref[0, t] = result
        if t + 1 < ticks:
            z_copy = send(
                out_ref.at[0, t], xbuf.at[t + 1, 0], z_send.at[t], z_recv.at[t], (nxt, me)
            )
            pending.append(z_copy)

    for copy in pending:
        copy.wait_send()


def local(
    hidden_entering,
    layer_norm_gain,
    query_matrix,
    output_matrix,
    adapter_down_weight,
    adapter_up_weight,
    key_value_cache,
    adapter_index,
    cached_lengths,
):
    sections = lax.axis_size("section")
    parts = lax.axis_size("tp")
    rows, share = hidden_entering.shape[1:]
    ticks, _, context, _ = key_value_cache.shape[1:]
    width, feats = query_matrix.shape[1:]
    adapters, rank_share = adapter_down_weight.shape[1:3]
    rank_full = adapter_up_weight.shape[2]
    vmem = pl.BlockSpec(memory_space=pltpu.VMEM)
    smem = pl.BlockSpec(memory_space=pltpu.SMEM)
    hbm = pl.BlockSpec(memory_space=pl.ANY)
    dma = pltpu.SemaphoreType.DMA
    return pl.pallas_call(
        functools.partial(kernel, sections, parts),
        out_shape=jax.ShapeDtypeStruct((1, ticks, rows, share), BF16),
        in_specs=[smem, smem, vmem, vmem, hbm, hbm, vmem, vmem, hbm],
        out_specs=vmem,
        scratch_shapes=[
            pltpu.VMEM((width, feats), BF16),
            pltpu.VMEM((feats, width), BF16),
            pltpu.VMEM((adapters * rank_share, width), F32),
            pltpu.VMEM((parts, adapters, rank_share, share), BF16),
            pltpu.VMEM((adapters * rank_full, share), F32),
            pltpu.VMEM((adapters * rank_full, share), BF16),
            pltpu.VMEM((adapters * rank_full, feats), BF16),
            pltpu.VMEM((ticks, rows, context, HD), BF16),
            pltpu.VMEM((ticks, rows, context, HD), BF16),
            pltpu.VMEM((ticks, parts, rows, share), BF16),
            pltpu.VMEM((parts, rows, share), BF16),
            pltpu.VMEM((ticks, parts, rows, adapters * rank_full), BF16),
            pltpu.VMEM((ticks, parts, rows, share), BF16),
            pltpu.VMEM((ticks, parts, rows, share), BF16),
            dma((parts + 1,)),
            dma((parts,)),
            dma((parts,)),
            dma((ticks, 2, parts)),
            dma((ticks, 2, parts)),
            dma((ticks, parts)),
            dma((ticks, parts)),
            dma((ticks, parts)),
            dma((ticks, parts)),
            dma((ticks, parts)),
            dma((ticks, parts)),
            dma((ticks,)),
            dma((ticks,)),
        ],
        compiler_params=pltpu.CompilerParams(
            collective_id=0, has_side_effects=True, vmem_limit_bytes=56 << 20
        ),
    )(
        adapter_index,
        cached_lengths,
        hidden_entering,
        layer_norm_gain,
        query_matrix,
        output_matrix,
        adapter_down_weight,
        adapter_up_weight,
        key_value_cache,
    )


def solution(mesh):
    placed = (
        P("section", None, "tp"),
        P("section", None),
        P("section", None, "tp"),
        P("section", "tp", None),
        P("section", None, "tp", None),
        P("section", None, None, "tp"),
        P("section", None, "tp", None, None),
        P(),
        P(),
    )
    return jax.shard_map(
        local, mesh=mesh, in_specs=placed, out_specs=P("section", None, None, "tp"), check_vma=False
    )
```

```python
import functools

import jax
import jax.numpy as jnp
from jax import lax
from jax.experimental import pallas as pl
from jax.experimental.pallas import tpu as pltpu
from jax.sharding import PartitionSpec as P

HD = 128
HEADS = 32
KVH = 4
ADAPTER_SCALE = 2.0
MESH = pl.DeviceIdType.MESH
BF16 = jnp.bfloat16
F32 = jnp.float32


def flipped(me, d):
    value, bit = me, 1
    while bit <= d:
        if d & bit:
            value = value + bit * (1 - 2 * ((me // bit) % 2))
        bit *= 2
    return value


def kernel(
    sections,
    parts,
    adapter_ref,
    lens_ref,
    x_ref,
    gain_ref,
    wq_hbm,
    wo_hbm,
    down_ref,
    up_ref,
    kv_hbm,
    out_ref,
    wq,
    wo,
    down32,
    dparts,
    dcols32,
    dcols,
    upbuf,
    kbuf,
    vbuf,
    xbuf,
    hbuf,
    ubuf,
    rbuf,
    sbuf,
    load_sem,
    d_send,
    d_recv,
    kv_send,
    kv_recv,
    x_send,
    x_recv,
    u_send,
    u_recv,
    r_send,
    r_recv,
    z_send,
    z_recv,
):
    section = lax.axis_index("section")
    me = lax.axis_index("tp")
    ticks = kbuf.shape[0]
    rows, share = x_ref.shape[1], x_ref.shape[2]
    width = parts * share
    owned = kv_hbm.shape[2]
    context = kv_hbm.shape[3]
    feats = wq.shape[1]
    heads = feats // HD
    group = HEADS // KVH
    adapters, rank_share = down_ref.shape[1], down_ref.shape[2]
    rank_full = up_ref.shape[2]
    ranks = adapters * rank_share
    nxt = (section + 1) % sections
    prv = (section + sections - 1) % sections

    wq_copies = []
    for d in range(parts):
        lo = pl.multiple_of(flipped(me, d) * share, share)
        wq_copies.append(
            pltpu.make_async_copy(
                wq_hbm.at[0, pl.ds(lo, share), :], wq.at[pl.ds(lo, share), :], load_sem.at[d]
            )
        )
    wo_copy = pltpu.make_async_copy(wo_hbm.at[0], wo, load_sem.at[parts])
    for copy in wq_copies:
        copy.start()
    wo_copy.start()

    barrier = pltpu.get_barrier_semaphore()
    for d in range(1, parts):
        pl.semaphore_signal(
            barrier, inc=1, device_id=(section, flipped(me, d)), device_id_type=MESH
        )
    pl.semaphore_signal(barrier, inc=1, device_id=(nxt, me), device_id_type=MESH)
    pl.semaphore_signal(barrier, inc=1, device_id=(prv, me), device_id_type=MESH)
    relayed = [d for d in range(2, parts, 2) if d >= parts - parts // 4]
    for d in relayed:
        for neighbour in (nxt, prv):
            pl.semaphore_signal(
                barrier, inc=1, device_id=(neighbour, flipped(me, d)), device_id_type=MESH
            )
    for a in range(adapters):
        down32[a * rank_share : (a + 1) * rank_share, :] = down_ref[0, a].astype(F32)
    xbuf[0, 0] = x_ref[0]
    pl.semaphore_wait(barrier, parts + 1 + 2 * len(relayed))

    def send(src, dst, ssem, rsem, device):
        copy = pltpu.make_async_remote_copy(
            src_ref=src,
            dst_ref=dst,
            send_sem=ssem,
            recv_sem=rsem,
            device_id=device,
            device_id_type=MESH,
        )
        copy.start()
        return copy

    far_first = list(range(parts - 1, 0, -1))
    via_partner = [d + 1 for d in relayed]
    direct = [d for d in far_first if d not in via_partner]
    near = [d for d in range(2, parts) if d not in relayed and d not in via_partner]
    near = [d for d in near if d % 2 == 0] + [d for d in near if d % 2 == 1]
    arrival = [0, 1] + relayed + near + via_partner
    partner = flipped(me, 1)
    pending = []
    x_ahead = {}

    def spread_x(t, src):
        copies = [None] * parts
        for d in direct:
            if t > 0 and d in relayed:
                copies[d] = x_ahead[d]
                continue
            copies[d] = send(
                src, xbuf.at[t, d], x_send.at[t, d], x_recv.at[t, d], (section, flipped(me, d))
            )
        pending.extend(c for c in copies if c is not None)
        return copies

    def spread_u(t):
        copies = [None] * parts
        for d in far_first:
            copies[d] = send(
                ubuf.at[t, 0],
                ubuf.at[t, d],
                u_send.at[t, d],
                u_recv.at[t, d],
                (section, flipped(me, d)),
            )
            pending.append(copies[d])
        return copies

    x_copies = spread_x(0, x_ref.at[0])

    def kv_head(device):
        return (device * heads) // group

    def rows_of(device):
        return pl.ds(pl.multiple_of(device * owned, owned), owned)

    kv_copies = {}

    def send_cache(t):
        for d in [0] + [e for e in far_first if e % 2 == 0] + [1]:
            peer = flipped(me, d)
            for i, buf in enumerate((kbuf, vbuf)):
                col = pl.multiple_of(i * KVH * HD + kv_head(peer) * HD, HD)
                src = kv_hbm.at[0, t, :, :, pl.ds(col, HD)]
                dst = buf.at[t, rows_of(me)]
                if d == 0:
                    copy = pltpu.make_async_copy(src, dst, kv_recv.at[t, i, 0])
                    copy.start()
                else:
                    copy = send(
                        src, dst, kv_send.at[t, i, d], kv_recv.at[t, i, d], (section, peer)
                    )
                    pending.append(copy)
                kv_copies[t, i, d] = copy

    def forward_cache(t):
        for d in range(2, parts, 2):
            for i, buf in enumerate((kbuf, vbuf)):
                kv_copies[t, i, d].wait_recv()
                block = buf.at[t, rows_of(flipped(me, d))]
                copy = send(
                    block,
                    block,
                    kv_send.at[t, i, d + 1],
                    kv_recv.at[t, i, d + 1],
                    (section, partner),
                )
                pending.append(copy)
                kv_copies[t, i, d + 1] = copy

    def wait_cache(t):
        for i in range(2):
            kv_copies[t, i, 0].wait()
            for d in range(1, parts):
                if d == 1 or d % 2 == 1:
                    kv_copies[t, i, d].wait_recv()

    d_copies = {}

    def send_down(peers):
        for d in peers:
            peer = flipped(me, d)
            lo = pl.multiple_of(peer * share, share)
            d_copies[d] = send(
                down_ref.at[0, :, :, pl.ds(lo, share)],
                dparts.at[me],
                d_send.at[d],
                d_recv.at[d],
                (section, peer),
            )
            pending.append(d_copies[d])

    down_first = [d for d in far_first if d >= parts - parts // 4 or d == 1]
    down_later = [d for d in far_first if d not in down_first]
    send_cache(0)
    my_cols = pl.ds(pl.multiple_of(me * share, share), share)
    dparts[me] = down_ref[0, :, :, my_cols]
    send_down(down_first)

    row = lax.broadcasted_iota(jnp.int32, (ranks, adapters * rank_full), 0)
    col = lax.broadcasted_iota(jnp.int32, (ranks, adapters * rank_full), 1)
    place = jnp.where(col == me * ranks + row, 1.0, 0.0).astype(BF16)
    full = adapters * rank_full
    row = lax.broadcasted_iota(jnp.int32, (full, full), 0)
    col = lax.broadcasted_iota(jnp.int32, (full, full), 1)
    source = (
        (row // rank_share) % adapters * rank_full + row // ranks * rank_share + row % rank_share
    )
    order = jnp.where(col == source, 1.0, 0.0).astype(BF16)
    up = jnp.dot(order, up_ref[0].reshape(full, feats), preferred_element_type=F32).astype(BF16)
    upbuf[...] = up

    for t in range(ticks):
        gidx = (section + sections - t) % sections
        r_id = lax.broadcasted_iota(jnp.int32, (rows, full), 0)
        a_id = lax.broadcasted_iota(jnp.int32, (rows, full), 1) // rank_share % adapters
        chosen = jnp.zeros((rows, full), jnp.int32)
        c_id = lax.broadcasted_iota(jnp.int32, (1, rows * context), 1)
        lens = jnp.zeros((1, rows * context), jnp.int32)
        for r in range(rows):
            chosen = jnp.where(r_id == r, adapter_ref[gidx, r], chosen)
            lens = jnp.where(c_id // context == r, lens_ref[gidx, r], lens)
        onehot = jnp.where(chosen == a_id, 1.0, 0.0)
        m_row = lax.broadcasted_iota(jnp.int32, (heads * rows, rows * context), 0) % rows
        m_col = lax.broadcasted_iota(jnp.int32, (heads * rows, rows * context), 1)
        valid = (m_row == m_col // context) & (m_col % context < lens)

        if t > 0:
            z_copy.wait_recv()
            x_copies = spread_x(t, xbuf.at[t, 0])
            h = (xbuf[t, 0].astype(F32) * gain_ref[:, my_cols].astype(F32)).astype(BF16)
            u_part = lax.dot_general(
                h, dcols[...], (((1,), (1,)), ((), ())), preferred_element_type=F32
            )
            ubuf[t, 0] = u_part.astype(BF16)
            u_copies = spread_u(t)

        squares = jnp.zeros((rows, 1), F32)
        acc_u = jnp.zeros((rows, ranks), F32)
        acc_q = jnp.zeros((rows, feats), F32)
        for k, d in enumerate(arrival):
            if d > 0:
                x_copies[d].wait_recv()
            if d in relayed:
                x_copies[d + 1] = send(
                    xbuf.at[t, d],
                    xbuf.at[t, d + 1],
                    x_send.at[t, d + 1],
                    x_recv.at[t, d + 1],
                    (section, partner),
                )
                pending.append(x_copies[d + 1])
            lo = pl.multiple_of(flipped(me, d) * share, share)
            xf = xbuf[t, d].astype(F32)
            squares += jnp.sum(xf * xf, axis=-1, keepdims=True)
            h = (xf * gain_ref[:, pl.ds(lo, share)].astype(F32)).astype(BF16)
            if t == 0:
                hbuf[d] = h
                acc_u += lax.dot_general(
                    h,
                    down32[:, pl.ds(lo, share)].astype(BF16),
                    (((1,), (1,)), ((), ())),
                    preferred_element_type=F32,
                )
            if t > 0 or k < parts // 2:
                if t == 0:
                    wq_copies[d].wait()
                acc_q += jnp.dot(h, wq[pl.ds(lo, share), :], preferred_element_type=F32)
        inv = lax.rsqrt(squares * (1.0 / width) + 1e-05)
        if t == 0:
            u_own = (acc_u * inv).astype(BF16)
            u_sum = jnp.dot(u_own, place, preferred_element_type=F32)
            ubuf[t, 0] = u_sum.astype(BF16)
            u_copies = spread_u(t)
            send_down(down_later)
            for d in arrival[parts // 2 :]:
                lo = pl.multiple_of(flipped(me, d) * share, share)
                wq_copies[d].wait()
                acc_q += jnp.dot(hbuf[d], wq[pl.ds(lo, share), :], preferred_element_type=F32)
        else:
            u_sum = u_part
        forward_cache(t)
        for d in range(1, parts):
            u_copies[d].wait_recv()
            u_sum += ubuf[t, d].astype(F32)
        if t > 0:
            u_sum = u_sum * inv
        u_sum = (u_sum * onehot).astype(BF16)
        delta = jnp.dot(u_sum, upbuf[...], preferred_element_type=F32)
        query = (acc_q * inv + ADAPTER_SCALE * delta).astype(BF16)

        wait_cache(t)
        qh = jnp.concatenate([query[:, i * HD : (i + 1) * HD] for i in range(heads)], axis=0)
        keys = kbuf[t].reshape(rows * context, HD)
        values = vbuf[t].reshape(rows * context, HD)
        scores = lax.dot_general(
            qh, keys, (((1,), (1,)), ((), ())), preferred_element_type=F32
        ) * HD ** (-0.5)
        scores = jnp.where(valid, scores, -1e30)
        top = jnp.max(scores, axis=-1, keepdims=True)
        expo = jnp.where(valid, jnp.exp(scores - top), 0.0)
        weights = (expo / jnp.sum(expo, axis=-1, keepdims=True)).astype(BF16)
        attn = jnp.dot(weights, values, preferred_element_type=F32).astype(BF16)
        attn = jnp.concatenate([attn[i * rows : (i + 1) * rows] for i in range(heads)], axis=1)

        if t == 0:
            wo_copy.wait()
        r_copies = [None] * parts

        def term(d):
            lo = pl.multiple_of(flipped(me, d) * share, share)
            return jnp.dot(attn, wo[:, pl.ds(lo, share)], preferred_element_type=F32).astype(BF16)

        def send_term(d, slot, device):
            r_copies[slot] = send(
                sbuf.at[t, d],
                rbuf.at[t, slot],
                r_send.at[t, slot],
                r_recv.at[t, slot],
                (section, device),
            )
            pending.append(r_copies[slot])

        for d in via_partner:
            sbuf[t, d] = term(d)
            send_term(d, d, partner)
        for d in near:
            sbuf[t, d] = term(d)
            send_term(d, d, flipped(me, d))
        for d in relayed:
            pair = term(d).astype(F32)
            r_copies[d + 1].wait_recv()
            sbuf[t, d] = (pair + rbuf[t, d + 1].astype(F32)).astype(BF16)
            send_term(d, d, flipped(me, d))
        sbuf[t, 1] = term(1)
        send_term(1, 1, partner)
        if t + 1 < ticks:
            send_cache(t + 1)
        total = (
            jnp.dot(attn, wo[:, my_cols], preferred_element_type=F32)
            .astype(BF16)
            .astype(F32)
        )
        if t == 0:
            for d in range(1, parts):
                d_copies[d].wait_recv()
            for p in range(parts):
                for a in range(adapters):
                    lo = p * ranks + a * rank_share
                    dcols32[lo : lo + rank_share, :] = dparts[p, a].astype(F32)
            dcols[...] = dcols32[...].astype(BF16)
        for d in [1] + near + relayed:
            r_copies[d].wait_recv()
            total += rbuf[t, d].astype(F32)
        result = (xbuf[t, 0].astype(F32) + total).astype(BF16)
        out_ref[0, t] = result
        if t + 1 < ticks:
            z_copy = send(
                out_ref.at[0, t], xbuf.at[t + 1, 0], z_send.at[t], z_recv.at[t], (nxt, me)
            )
            pending.append(z_copy)
            for d in relayed:
                x_ahead[d] = send(
                    out_ref.at[0, t],
                    xbuf.at[t + 1, d],
                    x_send.at[t + 1, d],
                    x_recv.at[t + 1, d],
                    (nxt, flipped(me, d)),
                )

    for copy in pending:
        copy.wait_send()


def local(
    hidden_entering,
    layer_norm_gain,
    query_matrix,
    output_matrix,
    adapter_down_weight,
    adapter_up_weight,
    key_value_cache,
    adapter_index,
    cached_lengths,
):
    sections = lax.axis_size("section")
    parts = lax.axis_size("tp")
    rows, share = hidden_entering.shape[1:]
    ticks, _, context, _ = key_value_cache.shape[1:]
    width, feats = query_matrix.shape[1:]
    adapters, rank_share = adapter_down_weight.shape[1:3]
    rank_full = adapter_up_weight.shape[2]
    vmem = pl.BlockSpec(memory_space=pltpu.VMEM)
    smem = pl.BlockSpec(memory_space=pltpu.SMEM)
    hbm = pl.BlockSpec(memory_space=pl.ANY)
    dma = pltpu.SemaphoreType.DMA
    return pl.pallas_call(
        functools.partial(kernel, sections, parts),
        out_shape=jax.ShapeDtypeStruct((1, ticks, rows, share), BF16),
        in_specs=[smem, smem, vmem, vmem, hbm, hbm, vmem, vmem, hbm],
        out_specs=vmem,
        scratch_shapes=[
            pltpu.VMEM((width, feats), BF16),
            pltpu.VMEM((feats, width), BF16),
            pltpu.VMEM((adapters * rank_share, width), F32),
            pltpu.VMEM((parts, adapters, rank_share, share), BF16),
            pltpu.VMEM((adapters * rank_full, share), F32),
            pltpu.VMEM((adapters * rank_full, share), BF16),
            pltpu.VMEM((adapters * rank_full, feats), BF16),
            pltpu.VMEM((ticks, rows, context, HD), BF16),
            pltpu.VMEM((ticks, rows, context, HD), BF16),
            pltpu.VMEM((ticks, parts, rows, share), BF16),
            pltpu.VMEM((parts, rows, share), BF16),
            pltpu.VMEM((ticks, parts, rows, adapters * rank_full), BF16),
            pltpu.VMEM((ticks, parts, rows, share), BF16),
            pltpu.VMEM((ticks, parts, rows, share), BF16),
            dma((parts + 1,)),
            dma((parts,)),
            dma((parts,)),
            dma((ticks, 2, parts)),
            dma((ticks, 2, parts)),
            dma((ticks, parts)),
            dma((ticks, parts)),
            dma((ticks, parts)),
            dma((ticks, parts)),
            dma((ticks, parts)),
            dma((ticks, parts)),
            dma((ticks,)),
            dma((ticks,)),
        ],
        compiler_params=pltpu.CompilerParams(
            collective_id=0, has_side_effects=True, vmem_limit_bytes=56 << 20
        ),
    )(
        adapter_index,
        cached_lengths,
        hidden_entering,
        layer_norm_gain,
        query_matrix,
        output_matrix,
        adapter_down_weight,
        adapter_up_weight,
        key_value_cache,
    )


def solution(mesh):
    placed = (
        P("section", None, "tp"),
        P("section", None),
        P("section", None, "tp"),
        P("section", "tp", None),
        P("section", None, "tp", None),
        P("section", None, None, "tp"),
        P("section", None, "tp", None, None),
        P(),
        P(),
    )
    return jax.shard_map(
        local, mesh=mesh, in_specs=placed, out_specs=P("section", None, None, "tp"), check_vma=False
    )
```
